32 devices in a mesh: days: 2 (over x), tm: 8 (over z, y), sta: 2 (over core).
Axes of the slice: x: 2, y: 2, z: 4, core: 2. Of those that a mesh axis runs over, the one named last changes fastest.
Arguments:
- records: bfloat16 [2048, 2048], P('sta', ('days', 'tm')), parts along dimension 1, may hold values from -6 to 6
- following: bfloat16 [2048, 510], P('sta', 'days'), parts along dimension 1, may hold values from -6 to 6
- library: bfloat16 [32, 2048, 256], P(None, ('sta', 'tm')), may hold values from -6 to 6
- template_ids: int32 [2, 8], replicated, may hold values from 0 to 31
- channel_mask: int32 [32, 2048], replicated, may hold values 0 or 1
- station_group: int32 [2048], replicated, may hold values from 0 to 127
Outputs:
- detection: float32 [2, 8, 2048], P('sta', None, ('days', 'tm')), parts along dimension 2
The draws below stay inside these ranges and needn't reach their ends.
There are 2 independent parts, one for each index of `days`. The reference program is written for one: setup_inputs(seed, part) draws one part's arguments, and reference() takes and returns one part's arrays. A program takes and returns all parts, laid end to end along the dimension named above; an argument that names none is the same for every part. Nothing has to cross between parts.
All inputs are finite; a program needn't handle non-finite values.
Results may differ from the reference program's by a relative error of at most 0.0003.
Values may be sent and summed in bfloat16 or wider, within the bound.
A program may use at most 128 MiB of HBM per device.

```python
import math
import jax
import jax.numpy as jnp
import numpy as np
from jax import lax

S = 2048
W = 256
NLIB = 32
NB = 2
KB = 8
G = 128
T_SIZE = 1024


def touch_ends(values, key, low, largest):
    longest = values.shape.index(max(values.shape))
    spots = []
    for shift in (0, 1):
        where = [jax.random.randint(jax.random.fold_in(key, axis), (), 0, length) for axis, length in enumerate(values.shape)]
        where[longest] = (where[longest] + shift) % values.shape[longest]
        spots.append(tuple(where))
    return values.at[spots[0]].set(low).at[spots[1]].set(largest)


def shard_levels(own_key, shape, pieces, least, largest):
    gain, own = 1.0, jax.random.fold_in(own_key, 6)
    for axis_at, blocks in pieces:
        steps = jnp.exp(jax.random.uniform(jax.random.fold_in(own, axis_at), (blocks,), jnp.float32, least / len(pieces), largest / len(pieces)))
        gain = gain * jnp.repeat(steps, shape[axis_at] // blocks).reshape([-1 if axis == axis_at else 1 for axis in range(len(shape))])
    return gain


def rank_bounds(number_of, skew):
    portions = [(1 << 20) // math.isqrt(grade ** skew) + 1 for grade in range(1, number_of + 1)]
    spread = 1 + sum(portions) // (1 << 30)
    return np.cumsum(np.array([max(1, weight // spread) for weight in portions]))


def skewed_ids(own_key, extent, number_of, lean):
    table = rank_bounds(number_of, lean)
    lot = jax.random.randint(jax.random.fold_in(own_key, 1), extent, 0, int(table[number_of - 1]))
    standing = jnp.searchsorted(jnp.asarray(table, jnp.int32), lot, side="right")
    return jax.random.permutation(jax.random.fold_in(own_key, 2), number_of)[standing].astype(jnp.int32)


def scatter_about(key, extent, spread, reach, split=(), kind=jnp.bfloat16):
    array = spread * jax.random.normal(key, extent, jnp.float32)
    if split:
        array = array * shard_levels(key, extent, split, -0.22, 0.18)
    return jnp.clip(array, -reach, reach).astype(kind)


def setup_inputs(seed: int = 0, part: int = 0) -> dict:
    key_of = jax.random.split(jax.random.key(seed), 7)
    part_splits = jax.random.split(jax.random.fold_in(key_of[6], part), 7)
    return {
        "records": scatter_about(part_splits[0], (S, T_SIZE), 1.0, 6.0, ((0, 2), (1, 8))),
        "following": scatter_about(part_splits[1], (S, W - 1), 1.0, 6.0, ((0, 2),)),
        "library": scatter_about(key_of[2], (NLIB, S, W), 1.0, 6.0, ((1, 16),)),
        "template_ids": touch_ends(jax.random.randint(key_of[3], (NB, KB), 0, NLIB), jax.random.fold_in(key_of[3], 1), 0, NLIB - 1).astype(jnp.int32),
        "channel_mask": touch_ends((jax.random.randint(key_of[4], (NLIB, S), 0, 2) < 1).astype(jnp.int32), jax.random.fold_in(key_of[4], 1), 0, 1),
        "station_group": touch_ends(skewed_ids(key_of[5], (S,), G, 2), jax.random.fold_in(key_of[5], 3), 0, G - 1).astype(jnp.int32),
    }


epsilon = 1e-06

def reference(records, following, library, template_ids, channel_mask, station_group):
    stream = jnp.concatenate([records, following], axis=1)
    squares = stream.astype(jnp.float32) ** 2
    energy = lax.reduce_window(squares, jnp.float32(0), lax.add, (1, W), (1, 1), 'VALID') / W
    inverse = 1.0 / jnp.sqrt(energy + epsilon)
    onehot = (station_group[:, None] == jnp.arange(G, dtype=jnp.int32)[None, :]).astype(jnp.int32)
    counts = jnp.dot(channel_mask, onehot, preferred_element_type=jnp.int32)
    per_station = jnp.take(counts, station_group, axis=1)
    tmean = lax.optimization_barrier(jnp.mean(library.astype(jnp.float32) ** 2, axis=2))
    coef = channel_mask.astype(jnp.float32) / jnp.sqrt(jnp.float32(W * G) * jnp.maximum(per_station, 1).astype(jnp.float32) * (tmean + epsilon))
    flat_ids = template_ids.reshape(-1)
    chosen = jnp.take(library, flat_ids, axis=0)
    weights = jnp.take(coef, flat_ids, axis=0)
    block_size = math.gcd(S, 16)
    grid = jnp.arange(W, dtype=jnp.int32)[:, None] + jnp.arange(T_SIZE, dtype=jnp.int32)[None, :]

    def advance(running, index):
        first = (index * block_size).astype(jnp.int32)
        rows = lax.dynamic_slice_in_dim(stream, first, block_size, 0)
        hankel = rows[:, grid].astype(jnp.float32)
        temps = lax.dynamic_slice_in_dim(chosen, first, block_size, 1).astype(jnp.float32)
        corr = jnp.einsum('jbw,bwt->jbt', temps, hankel)
        weight = lax.dynamic_slice_in_dim(weights, first, block_size, 1)
        scale = lax.dynamic_slice_in_dim(inverse, first, block_size, 0)
        return (running + lax.optimization_barrier(jnp.sum(corr * weight[:, :, None] * scale[None], axis=1)), None)
    start_zero = jnp.zeros((NB * KB, T_SIZE), jnp.float32)
    result = lax.scan(advance, start_zero, jnp.arange(S // block_size, dtype=jnp.int32))[0]
    return result.reshape(NB, KB, T_SIZE)
```

```python
import functools

import jax
import jax.numpy as jnp
from jax import lax
from jax.experimental import pallas as pl
from jax.experimental.pallas import tpu as pltpu
from jax.sharding import PartitionSpec as P

G = 128
LANES = 128
HOP = 8
FRAMES = LANES // HOP
PIECE = 32

epsilon = 1e-06

f32, bf16 = jnp.float32, jnp.bfloat16
NT = (((1,), (1,)), ((), ()))


def iota(shape, axis):
    return lax.broadcasted_iota(jnp.int32, shape, axis)


def as_bf16(mask):
    return mask.astype(f32).astype(bf16)


def split(x, count):
    pieces = []
    for _ in range(count):
        piece = x.astype(bf16)
        pieces.append(piece)
        x = x - piece.astype(f32)
    return pieces


def swap_blocks(tiles):
    block = iota(tiles[0].shape, 1) // FRAMES
    step = 1
    while step < len(tiles):
        odd = (block // step) % 2 == 1
        turned = list(tiles)
        for a in range(len(tiles)):
            if a & step == 0:
                low, high = tiles[a], tiles[a | step]
                turned[a] = jnp.where(odd, pltpu.roll(high, FRAMES * step, 1), low)
                turned[a | step] = jnp.where(odd, high, pltpu.roll(low, LANES - FRAMES * step, 1))
        tiles = turned
        step *= 2
    return tiles


def station_weights(ids, first, window, mask_ref, group_ref):
    stations = mask_ref.shape[1]
    turn = lax.rem(stations - first, stations)
    mask = jnp.concatenate([mask_ref[pl.ds(i, 1), :] for i in ids], axis=0).astype(f32)
    names = group_ref[...]
    onehot = iota((G, stations), 0) == jnp.broadcast_to(names, (G, stations))
    counts = lax.dot_general(mask.astype(bf16), as_bf16(onehot), NT, preferred_element_type=f32)
    mine = pltpu.roll(jnp.broadcast_to(names, (8, stations)), turn, 1)[:1, :LANES]
    chosen = as_bf16(iota((G, LANES), 0) == jnp.broadcast_to(mine, (G, LANES)))
    high = jnp.floor(counts / 128.0) * 128.0
    low = counts - high
    per_station = jnp.dot(high.astype(bf16), chosen, preferred_element_type=f32) + jnp.dot(
        low.astype(bf16), chosen, preferred_element_type=f32
    )
    my_mask = pltpu.roll(mask, turn, 1)[:, :LANES]
    return my_mask * lax.rsqrt(jnp.float32(window * G) * jnp.maximum(per_station, 1.0))


def pad_rows(x):
    if x.shape[0] == LANES:
        return x
    return jnp.concatenate([x, jnp.zeros((LANES - x.shape[0], x.shape[1]), x.dtype)], axis=0)


def prepare_templates(ids, weights, templates, temps, coef, taps, ends):
    slots, wide, rows, _ = temps.shape
    window = wide * LANES
    lane = iota((rows, LANES), 1)
    select = as_bf16(iota((16, LANES), 1) + iota((16, LANES), 0) == LANES)
    mean = jnp.zeros((rows, LANES), f32)
    for k in range(slots):
        template = templates[ids[k]]
        last = lax.dot_general(select, pad_rows(template[:, window - LANES :]), NT, preferred_element_type=f32)
        taps[pl.ds(k, HOP, stride=slots), :] = last[:HOP]
        template = template.astype(f32)
        for a in range(wide):
            temps[k, a] = template[:, a * LANES : (a + 1) * LANES]
        total = jnp.sum(template * template, axis=1, keepdims=True)
        mean = jnp.where(lane == k, total, mean)
    mean = pad_rows(mean).T[:slots]
    own = weights * lax.rsqrt(mean / window + epsilon)
    pieces = jnp.concatenate(split(own, 3), axis=0)
    repeat = as_bf16(lax.rem(iota((3 * slots, slots * LANES), 0), slots) == iota((3 * slots, slots * LANES), 1) // LANES)
    spread = lax.dot_general(pieces, repeat, (((0,), (0,)), ((), ())), preferred_element_type=f32)
    for k in range(slots):
        coef[k] = spread[:rows, k * LANES : (k + 1) * LANES]
    for g in range(rows // PIECE):
        tiles = [jnp.zeros((slots, LANES), f32)] * (HOP * PIECE // LANES)
        for d in range(1, HOP):
            place = (HOP - d) * PIECE
            part = taps[d * slots : (d + 1) * slots, :] * own
            part = pltpu.roll(part, (place - g * PIECE) % LANES, 1)
            at = place // LANES
            here = iota((slots, LANES), 1) // PIECE == (place % LANES) // PIECE
            tiles[at] = jnp.where(here, part, tiles[at])
        ends[g] = jnp.concatenate(split(jnp.concatenate(tiles, axis=1), 2), axis=0)


def build_shifts(temps, shifts):
    slots, wide, rows, _ = temps.shape
    keep = iota((HOP, LANES), 1) >= iota((HOP, LANES), 0)
    batch = min(8, rows)

    def build(step, carry):
        for b in range(batch):
            s = step * batch + b
            columns = [[] for _ in range(wide)]
            for k in range(slots):
                before = jnp.zeros((HOP, LANES), f32)
                for a in range(wide):
                    turned = pltpu.roll(temps[k, a, pl.ds(s, HOP, stride=0), :], 0, 1, stride=1, stride_axis=0)
                    columns[a].append(jnp.where(keep, turned, before))
                    before = turned
            for a in range(wide):
                shifts[s, a] = jnp.concatenate(columns[a], axis=0).astype(bf16)
        return carry

    lax.fori_loop(0, rows // batch, build, 0)


def phase_order():
    t, lane = iota((LANES, LANES), 0), iota((LANES, LANES), 1)
    return as_bf16(t == HOP * (FRAMES - 1 - lane % FRAMES) + lane // FRAMES)


def frame_at(lane):
    return lane // FRAMES * FRAMES + FRAMES - 1 - lane % FRAMES


def band_matrix(wide):
    shape = (2 * LANES, 2 * LANES)
    late = frame_at(iota(shape, 0)) - frame_at(iota(shape, 1) % LANES) - iota(shape, 1) // LANES
    return as_bf16(jnp.logical_and(late >= 0, late < wide * FRAMES))


def stretch_matrix():
    row, lane = iota((LANES, HOP * LANES), 0), iota((LANES, HOP * LANES), 1)
    same = row // FRAMES == lane // LANES
    return as_bf16(jnp.logical_and(same, lane % LANES // HOP == FRAMES - 1 - row % FRAMES))


def scales(tiles, window, order, band, level, at):
    chunk = len(tiles) - window // LANES
    wide = window // LANES
    stations = tiles[0].shape[0]
    mixed = jnp.dot(jnp.concatenate(tiles, axis=0), order, preferred_element_type=f32)
    mixed = [mixed[m * stations : (m + 1) * stations] for m in range(len(tiles))]
    main = swap_blocks(mixed[:chunk])
    lane = iota((stations, LANES), 1)
    rest = []
    for p in range(HOP):
        tail = None
        for a in range(wide):
            shift = (FRAMES * (a - p)) % LANES
            moved = pltpu.roll(mixed[chunk + a], shift, 1) if shift else mixed[chunk + a]
            tail = moved if tail is None else jnp.where(lane // FRAMES == a, moved, tail)
        rest.append(tail)
    squares = [jnp.concatenate([m * m, r * r], axis=1) for m, r in zip(main, rest)]
    pieces = [split(square, 2) for square in squares]
    sums = jnp.dot(
        jnp.concatenate([high for high, _ in pieces] + [low for _, low in pieces], axis=0),
        band[...],
        preferred_element_type=f32,
    )
    count = HOP * stations
    sums = sums[:count] + sums[count:]
    here = [sums[p * stations : (p + 1) * stations, :LANES] for p in range(HOP)]
    then = [sums[p * stations : (p + 1) * stations, LANES:] for p in range(HOP)]
    after = [None] * HOP
    for p in reversed(range(HOP)):
        after[p] = here[p] if p == HOP - 1 else here[p] + after[p + 1]
    ahead = None
    scale = []
    for j in range(HOP):
        energy = after[j] if ahead is None else after[j] + ahead
        ahead = then[j] if ahead is None else ahead + then[j]
        scale.append(lax.rsqrt(energy / window + epsilon))
        level[pl.ds(at + j, stations, stride=HOP), :] = scale[j]
    shift = LANES - wide * FRAMES
    behind = [
        jnp.where(lane < shift, pltpu.roll(main[p], shift, 1), pltpu.roll(rest[p], shift, 1)) for p in range(HOP - 1)
    ]
    return scale, behind


def end_taps(scale, behind, ends):
    slots = ends.shape[0] // 2
    stations = scale[0].shape[0]
    zero = jnp.zeros((stations, LANES), f32)
    sums = []
    for j in range(1, HOP):
        blocks = HOP if j > HOP // 2 else HOP // 2
        parts = [scale[j] * behind[j - d] if d <= j else zero for d in range(blocks, 0, -1)]
        high, low = split(jnp.concatenate(parts, axis=0), 2)
        left = ends[:, (HOP - blocks) * stations :]
        some = jnp.dot(left, high, preferred_element_type=f32)
        more = jnp.dot(left[:slots], low, preferred_element_type=f32)
        sums.append(some[:slots] + some[slots:] + more)
    return sums


def kernel(
    count, halves,
    ids_ref, records_ref, following_ref, library_ref, mask_ref, group_ref,
    out_ref,
    held, tail, templates, temps, shifts, stream, level, coef, taps, ends, order, band, stretch,
    acc, late, parts, arrived,
    own_sem, send_sem, recv_sem, out_send_sem, out_recv_sem,
):
    me, core = lax.axis_index("tm"), lax.axis_index("sta")
    slots, wide, rows, _ = temps.shape
    window = wide * LANES
    block_len = held.shape[2]
    tiles = count * block_len // LANES
    chunk = LANES // FRAMES
    offset = pl.multiple_of(me * rows, rows)

    pull = pltpu.make_async_copy(library_ref, templates, own_sem.at[0])
    own = pltpu.make_async_copy(records_ref.at[pl.ds(offset, rows), :], held.at[me], own_sem.at[1])
    after = pltpu.make_async_copy(following_ref.at[pl.ds(offset, rows), :], tail, own_sem.at[2])
    pull.start()
    own.start()
    after.start()

    others = [lax.rem(me + step, count) for step in range(1, count)]
    everyone = [(other, core) for other in others]
    everyone += [
        (lax.rem(me + step, count), lax.rem(core + turn, halves)) for turn in range(1, halves) for step in range(count)
    ]
    barrier = pltpu.get_barrier_semaphore()
    for b, h in everyone:
        pl.semaphore_signal(barrier, inc=1, device_id={"tm": b, "sta": h}, device_id_type=pl.DeviceIdType.MESH)

    ids = [ids_ref[j // ids_ref.shape[1], j % ids_ref.shape[1]] for j in range(slots)]
    first = core * (rows * count) + offset
    weights = station_weights(ids, first, window, mask_ref, group_ref)

    pl.semaphore_wait(barrier, len(everyone))

    def piece_copy(g, step, other):
        return pltpu.make_async_remote_copy(
            src_ref=records_ref.at[pl.ds(pl.multiple_of(other * rows + g * PIECE, PIECE), PIECE), :],
            dst_ref=held.at[me, pl.ds(pl.multiple_of(g * PIECE, PIECE), PIECE), :],
            send_sem=send_sem.at[g, step],
            recv_sem=recv_sem.at[g, step],
            device_id={"tm": other},
            device_id_type=pl.DeviceIdType.MESH,
        )

    for g in range(rows // PIECE):
        for step, other in enumerate(others):
            piece_copy(g, step, other).start()

    order[...] = phase_order()
    band[...] = band_matrix(wide)
    stretch[...] = stretch_matrix()
    acc[...] = jnp.zeros(acc.shape, f32)
    late[...] = jnp.zeros(late.shape, f32)
    pull.wait()
    prepare_templates(ids, weights, templates, temps, coef, taps, ends)
    build_shifts(temps, shifts)
    after.wait()
    for a in range(wide):
        width = min(LANES, tail.shape[1] - a * LANES)
        stream[tiles + a] = jnp.zeros((rows, LANES), f32)
        stream[tiles + a, :, :width] = tail[:, a * LANES : a * LANES + width].astype(f32)
    own.wait()

    inside = iota((FRAMES, LANES), 1) < LANES - HOP * (FRAMES - 1 - iota((FRAMES, LANES), 0))

    def piece(g, carry):
        for step, other in enumerate(others):
            piece_copy(g, step, other).wait()
        base = pl.multiple_of(g * PIECE, PIECE)
        span = pl.ds(base, PIECE)
        columns = []
        for m in range(tiles):
            at = m * LANES % block_len
            columns.append(held[m * LANES // block_len, span, at : at + LANES])
            stream[m, span, :] = columns[m].astype(f32)
        for a in range(wide):
            columns.append(stream[tiles + a, span, :].astype(bf16))
        for c in range(tiles // chunk):
            scale, behind = scales(
                columns[c * chunk : (c + 1) * chunk + wide], window, order[...], band, level, base * HOP
            )
            for j, part in enumerate(end_taps(scale, behind, ends[g])):
                late[c, j + 1] += part
            sums = [None] * slots
            for b in range(PIECE):
                s = base + b
                turned = [
                    pltpu.roll(stream[c * chunk + m, pl.ds(s, FRAMES, stride=0), :], HOP, 1, stride=HOP, stride_axis=0)
                    for m in range(chunk + wide)
                ]
                frames = [
                    jnp.where(inside, turned[m], turned[m + 1]).astype(bf16) for m in range(chunk + wide - 1)
                ]
                right = jnp.concatenate(
                    [jnp.concatenate(frames[a : a + chunk], axis=0) for a in range(wide)], axis=1
                )
                left = jnp.concatenate([shifts[s, a] for a in range(wide)], axis=1)
                corr = lax.dot_general(left, right, NT, preferred_element_type=f32)
                own_level = level[pl.ds(pl.multiple_of(base * HOP + b * HOP, HOP), HOP), :]
                for k in range(slots):
                    weight = own_level * coef[k, pl.ds(s, HOP, stride=0), :]
                    term = corr[k * HOP : (k + 1) * HOP] * weight
                    sums[k] = term if sums[k] is None else sums[k] + term
            for k in range(slots):
                acc[c, k * HOP : (k + 1) * HOP, :] += sums[k]
        return carry

    lax.fori_loop(0, rows // PIECE, piece, 0)

    per_half = slots // halves
    for c in range(tiles // chunk):
        for j in range(1, HOP):
            acc[c, pl.ds(j, slots, stride=HOP), :] += late[c, j]
        for h in range(halves):
            whole = [acc[c, k * HOP : (k + 1) * HOP, :] for k in range(h * per_half, (h + 1) * per_half)]
            for m, part in enumerate(swap_blocks(whole)):
                parts[c * chunk + m, h] = part

    sends = []
    per = tiles // count
    for step, (b, h) in enumerate(everyone):
        copy = pltpu.make_async_remote_copy(
            src_ref=parts.at[pl.ds(b * per, per), h],
            dst_ref=arrived.at[step],
            send_sem=out_send_sem.at[step],
            recv_sem=out_recv_sem.at[step],
            device_id={"tm": b, "sta": h},
            device_id_type=pl.DeviceIdType.MESH,
        )
        copy.start()
        sends.append(copy)
    total = parts[pl.ds(me * per, per), core]
    for step, copy in enumerate(sends):
        copy.wait_recv()
        total = total + arrived[step]
    mine = iota((HOP, LANES), 1) % HOP == iota((HOP, LANES), 0)
    for p in range(per):
        pieces = jnp.concatenate([piece.astype(f32) for piece in split(total[p], 3)], axis=0).astype(bf16)
        wider = jnp.dot(pieces, stretch[...], preferred_element_type=f32)
        wider = wider[:HOP] + wider[HOP : 2 * HOP] + wider[2 * HOP :]
        for k in range(per_half):
            line = jnp.where(mine, wider[:, k * LANES : (k + 1) * LANES], 0.0)
            out_ref[0, k : k + 1, p * LANES : (p + 1) * LANES] = jnp.sum(line, axis=0, keepdims=True)
    for copy in sends:
        copy.wait_send()


def shards(count, halves, records, following, library, template_ids, channel_mask, station_group):
    block_len = records.shape[1]
    rows, window = library.shape[1:]
    batches, per_batch = template_ids.shape
    slots = template_ids.size
    wide = window // LANES
    tiles = count * block_len // LANES
    chunks = tiles * FRAMES // LANES
    peers = count * halves - 1
    pieces = rows // PIECE
    return pl.pallas_call(
        functools.partial(kernel, count, halves),
        in_specs=[pl.BlockSpec(memory_space=pltpu.SMEM)]
        + [pl.BlockSpec(memory_space=pl.ANY)] * 3
        + [pl.BlockSpec(memory_space=pltpu.VMEM)] * 2,
        out_specs=pl.BlockSpec(memory_space=pltpu.VMEM),
        out_shape=jax.ShapeDtypeStruct((batches // halves, per_batch, block_len), f32),
        scratch_shapes=[
            pltpu.VMEM((count, rows, block_len), records.dtype),
            pltpu.VMEM((rows, following.shape[1]), following.dtype),
            pltpu.VMEM(library.shape, library.dtype),
            pltpu.VMEM((slots, wide, rows, LANES), f32),
            pltpu.VMEM((rows, wide, slots * HOP, LANES), bf16),
            pltpu.VMEM((tiles + wide, rows, LANES), f32),
            pltpu.VMEM((rows * HOP, LANES), f32),
            pltpu.VMEM((slots, rows, LANES), f32),
            pltpu.VMEM((HOP * slots, LANES), f32),
            pltpu.VMEM((pieces, 2 * slots, HOP * PIECE), bf16),
            pltpu.VMEM((LANES, LANES), bf16),
            pltpu.VMEM((2 * LANES, 2 * LANES), bf16),
            pltpu.VMEM((LANES, HOP * LANES), bf16),
            pltpu.VMEM((chunks, slots * HOP, LANES), f32),
            pltpu.VMEM((chunks, HOP, slots, LANES), f32),
            pltpu.VMEM((tiles, halves, HOP, LANES), f32),
            pltpu.VMEM((peers, tiles // count, HOP, LANES), f32),
            pltpu.SemaphoreType.DMA((3,)),
            pltpu.SemaphoreType.DMA((pieces, count - 1)),
            pltpu.SemaphoreType.DMA((pieces, count - 1)),
            pltpu.SemaphoreType.DMA((peers,)),
            pltpu.SemaphoreType.DMA((peers,)),
        ],
        compiler_params=pltpu.CompilerParams(collective_id=0, has_side_effects=True),
        name="matched_filter",
    )(template_ids, records, following, library, channel_mask, station_group.reshape(1, -1))


def solution(mesh):
    placed = (
        P("sta", ("days", "tm")),
        P("sta", "days"),
        P(None, ("sta", "tm"), None),
        P(),
        P(),
        P(),
    )
    return jax.shard_map(
        functools.partial(shards, mesh.shape["tm"], mesh.shape["sta"]),
        mesh=mesh,
        in_specs=placed,
        out_specs=P("sta", None, ("days", "tm")),
        check_vma=False,
    )
```

```python
import functools

import jax
import jax.numpy as jnp
from jax import lax
from jax.experimental import pallas as pl
from jax.experimental.pallas import tpu as pltpu
from jax.sharding import PartitionSpec as P

G = 128
LANES = 128
HOP = 8
FRAMES = LANES // HOP
PAIR = 2
PIECE = 32
EARLY = 2

epsilon = 1e-06

f32, bf16 = jnp.float32, jnp.bfloat16
NT = (((1,), (1,)), ((), ()))


def iota(shape, axis):
    return lax.broadcasted_iota(jnp.int32, shape, axis)


def as_bf16(mask):
    return mask.astype(f32).astype(bf16)


def split(x, count):
    pieces = []
    for _ in range(count):
        piece = x.astype(bf16)
        pieces.append(piece)
        x = x - piece.astype(f32)
    return pieces


def swap_blocks(tiles):
    block = iota(tiles[0].shape, 1) // FRAMES
    step = 1
    while step < len(tiles):
        odd = (block // step) % 2 == 1
        turned = list(tiles)
        for a in range(len(tiles)):
            if a & step == 0:
                low, high = tiles[a], tiles[a | step]
                turned[a] = jnp.where(odd, pltpu.roll(high, FRAMES * step, 1), low)
                turned[a | step] = jnp.where(odd, high, pltpu.roll(low, LANES - FRAMES * step, 1))
        tiles = turned
        step *= 2
    return tiles


def station_weights(ids, first, window, mask_ref, group_ref):
    stations = mask_ref.shape[1]
    turn = lax.rem(stations - first, stations)
    mask = jnp.concatenate([mask_ref[pl.ds(i, 1), :] for i in ids], axis=0).astype(f32)
    names = group_ref[...]
    onehot = iota((G, stations), 0) == jnp.broadcast_to(names, (G, stations))
    counts = lax.dot_general(mask.astype(bf16), as_bf16(onehot), NT, preferred_element_type=f32)
    mine = pltpu.roll(jnp.broadcast_to(names, (8, stations)), turn, 1)[:1, :LANES]
    chosen = as_bf16(iota((G, LANES), 0) == jnp.broadcast_to(mine, (G, LANES)))
    high = jnp.floor(counts / 128.0) * 128.0
    low = counts - high
    per_station = jnp.dot(high.astype(bf16), chosen, preferred_element_type=f32) + jnp.dot(
        low.astype(bf16), chosen, preferred_element_type=f32
    )
    my_mask = pltpu.roll(mask, turn, 1)[:, :LANES]
    return my_mask * lax.rsqrt(jnp.float32(window * G) * jnp.maximum(per_station, 1.0))


def pad_rows(x):
    if x.shape[0] == LANES:
        return x
    return jnp.concatenate([x, jnp.zeros((LANES - x.shape[0], x.shape[1]), x.dtype)], axis=0)


def spread_templates(ids, templates, temps, taps):
    slots, wide, rows, _ = temps.shape
    window = wide * LANES
    lane = iota((rows, LANES), 1)
    select = as_bf16(iota((16, LANES), 1) + iota((16, LANES), 0) == LANES)
    mean = jnp.zeros((rows, LANES), f32)
    for k in range(slots):
        template = templates[ids[k]]
        last = lax.dot_general(select, pad_rows(template[:, window - LANES :]), NT, preferred_element_type=f32)
        taps[pl.ds(k, HOP, stride=slots), :] = last[:HOP]
        template = template.astype(f32)
        for a in range(wide):
            temps[k, a] = template[:, a * LANES : (a + 1) * LANES]
        total = jnp.sum(template * template, axis=1, keepdims=True)
        mean = jnp.where(lane == k, total, mean)
    return mean


def weigh_templates(weights, mean, temps, coef, taps, ends):
    slots, wide, rows, _ = temps.shape
    window = wide * LANES
    mean = pad_rows(mean).T[:slots]
    own = weights * lax.rsqrt(mean / window + epsilon)
    pieces = jnp.concatenate(split(own, 3), axis=0)
    repeat = as_bf16(lax.rem(iota((3 * slots, slots * LANES), 0), slots) == iota((3 * slots, slots * LANES), 1) // LANES)
    spread = lax.dot_general(pieces, repeat, (((0,), (0,)), ((), ())), preferred_element_type=f32)
    for k in range(slots):
        coef[k] = spread[:rows, k * LANES : (k + 1) * LANES]
    for g in range(rows // PIECE):
        tiles = [jnp.zeros((slots, LANES), f32)] * (HOP * PIECE // LANES)
        for d in range(1, HOP):
            place = (HOP - d) * PIECE
            part = taps[d * slots : (d + 1) * slots, :] * own
            part = pltpu.roll(part, (place - g * PIECE) % LANES, 1)
            at = place // LANES
            here = iota((slots, LANES), 1) // PIECE == (place % LANES) // PIECE
            tiles[at] = jnp.where(here, part, tiles[at])
        ends[g] = jnp.concatenate(split(jnp.concatenate(tiles, axis=1), 2), axis=0)


def build_shifts(temps, shifts, stations):
    slots, wide = temps.shape[:2]
    keep = iota((HOP, LANES), 1) >= iota((HOP, LANES), 0)
    for s in stations:
        columns = [[] for _ in range(wide)]
        for k in range(slots):
            before = jnp.zeros((HOP, LANES), f32)
            for a in range(wide):
                turned = pltpu.roll(temps[k, a, pl.ds(s, HOP, stride=0), :], 0, 1, stride=1, stride_axis=0)
                columns[a].append(jnp.where(keep, turned, before))
                before = turned
        for a in range(wide):
            shifts[s, a] = jnp.concatenate(columns[a], axis=0).astype(bf16)


def sample_at(lane):
    return HOP * (FRAMES - 1 - lane % FRAMES) + lane // FRAMES


def phase_order():
    return as_bf16(iota((LANES, LANES), 0) == sample_at(iota((LANES, LANES), 1)))


def band_matrix(window):
    shape = (window + 2 * LANES, 2 * LANES)
    column = iota(shape, 1)
    late = iota(shape, 0) - column // LANES * LANES - sample_at(column % LANES)
    return as_bf16(jnp.logical_and(late >= 0, late < window))


def stretch_matrix():
    row, lane = iota((LANES, HOP * LANES), 0), iota((LANES, HOP * LANES), 1)
    same = row // FRAMES == lane // LANES
    return as_bf16(jnp.logical_and(same, lane % LANES // HOP == FRAMES - 1 - row % FRAMES))


def scales(tiles, window, order, band, level, at):
    wide = window // LANES
    chunk = len(tiles) - wide
    stations = tiles[0].shape[0]
    mixed = jnp.dot(jnp.concatenate(tiles[wide:], axis=0), order, preferred_element_type=f32).astype(bf16)
    behind = swap_blocks([mixed[m * stations : (m + 1) * stations] for m in range(chunk)])
    squares = [tile.astype(f32) * tile.astype(f32) for tile in tiles]
    pieces = [split(square, 2) for square in squares]
    rows = [
        jnp.concatenate([pieces[m + a][half] for a in range(wide + 2)], axis=1)
        for half in range(2)
        for m in range(0, chunk, 2)
    ]
    sums = jnp.dot(jnp.concatenate(rows, axis=0), band[...], preferred_element_type=f32)
    count = chunk // 2 * stations
    scale = lax.rsqrt((sums[:count] + sums[count:]) / window + epsilon)
    scale = swap_blocks(
        [
            scale[m // 2 * stations : (m // 2 + 1) * stations, m % 2 * LANES : (m % 2 + 1) * LANES]
            for m in range(chunk)
        ]
    )
    for j in range(HOP):
        level[pl.ds(at + j, stations, stride=HOP), :] = scale[j]
    return scale, [part.astype(f32) for part in behind[: HOP - 1]]


def end_taps(scale, behind, ends):
    slots = ends.shape[0] // 2
    stations = scale[0].shape[0]
    zero = jnp.zeros((stations, LANES), f32)
    sums = []
    for j in range(1, HOP):
        blocks = HOP if j > HOP // 2 else HOP // 2
        parts = [scale[j] * behind[j - d] if d <= j else zero for d in range(blocks, 0, -1)]
        high, low = split(jnp.concatenate(parts, axis=0), 2)
        left = ends[:, (HOP - blocks) * stations :]
        some = jnp.dot(left, high, preferred_element_type=f32)
        more = jnp.dot(left[:slots], low, preferred_element_type=f32)
        sums.append(some[:slots] + some[slots:] + more)
    return sums


def kernel(
    count, halves,
    ids_ref, records_ref, following_ref, library_ref, mask_ref, group_ref,
    out_ref,
    ids_own, mask_own, group_own, held, tail, templates, temps, shifts, stream, level, coef, taps, ends,
    order, band, stretch, acc, late, parts, arrived,
    own_sem, meet_sem, send_sem, recv_sem, out_send_sem, out_recv_sem,
):
    me, core = lax.axis_index("tm"), lax.axis_index("sta")
    slots, wide, rows, _ = temps.shape
    window = wide * LANES
    block_len = held.shape[2]
    tiles = count * block_len // LANES
    chunk = LANES // FRAMES
    offset = pl.multiple_of(me * rows, rows)

    local = [
        pltpu.make_async_copy(ids_ref, ids_own, own_sem.at[0]),
        pltpu.make_async_copy(mask_ref, mask_own, own_sem.at[1]),
        pltpu.make_async_copy(group_ref, group_own, own_sem.at[2]),
        pltpu.make_async_copy(library_ref, templates, own_sem.at[3]),
        pltpu.make_async_copy(records_ref.at[pl.ds(offset, rows), :], held.at[me], own_sem.at[4]),
        pltpu.make_async_copy(following_ref.at[pl.ds(offset, rows), :], tail, own_sem.at[5]),
    ]
    for copy in local:
        copy.start()

    line = count // PAIR
    place, side = me // PAIR, lax.rem(me, PAIR)
    hops = [(None, me, lax.rem(core + turn, halves)) for turn in range(1, halves)]
    hops += [(None, place * PAIR + lax.rem(side + turn, PAIR), core) for turn in range(1, PAIR)]
    hops += [(place > 0, me - PAIR, core), (place < line - 1, me + PAIR, core)]
    degree = halves + PAIR - 2 + (place > 0).astype(jnp.int32) + (place < line - 1).astype(jnp.int32)

    def meeting(turn):
        return pltpu.get_barrier_semaphore() if turn == 0 else meet_sem.at[turn - 1]

    def greet(turn):
        for there, b, h in hops:
            def signal():
                pl.semaphore_signal(
                    meeting(turn), inc=1, device_id={"tm": b, "sta": h}, device_id_type=pl.DeviceIdType.MESH
                )
            if there is None:
                signal()
            else:
                pl.when(there)(signal)

    def meet(turn):
        pl.semaphore_wait(meeting(turn), degree)

    def records_copy(other, sender):
        return pltpu.make_async_remote_copy(
            src_ref=records_ref.at[pl.ds(pl.multiple_of(other * rows, rows), rows), :],
            dst_ref=held.at[sender],
            send_sem=send_sem.at[other],
            recv_sem=recv_sem.at[sender],
            device_id={"tm": other},
            device_id_type=pl.DeviceIdType.MESH,
        )

    def send(distance):
        for turn in range(PAIR):
            far = distance - (turn > 0)
            for step in sorted({far, -far}):
                if 0 <= far < line and (turn, step) != (0, 0):
                    other = (place + step) * PAIR + lax.rem(side + turn, PAIR)

                    def start(other=other):
                        records_copy(other, me).start()

                    if step == 0:
                        start()
                    else:
                        pl.when(jnp.logical_and(place + step >= 0, place + step < line))(start)

    greet(0)
    order[...] = phase_order()
    band[...] = band_matrix(window)
    stretch[...] = stretch_matrix()
    acc[...] = jnp.zeros(acc.shape, f32)
    late[...] = jnp.zeros(late.shape, f32)
    meet(0)
    greet(1)
    send(1)
    for copy in local[:3]:
        copy.wait()
    ids = [ids_own[j // ids_own.shape[1], j % ids_own.shape[1]] for j in range(slots)]
    first = core * (rows * count) + offset
    weights = station_weights(ids, first, window, mask_own, group_own)
    meet(1)
    greet(2)
    send(2)
    local[3].wait()
    mean = spread_templates(ids, templates, temps, taps)
    for turn in range(2, line + 1):
        meet(turn)
        if turn < line:
            greet(turn + 1)
            send(turn + 1)
        if turn == 2:
            weigh_templates(weights, mean, temps, coef, taps, ends)

    pieces = rows // PIECE
    stations = [range(g * PIECE, (g + 1) * PIECE) for g in range(pieces)]
    early = min(EARLY, pieces)
    for g in range(early):
        build_shifts(temps, shifts, stations[g])
    local[5].wait()
    for a in range(wide):
        width = min(LANES, tail.shape[1] - a * LANES)
        stream[tiles + a] = jnp.zeros((rows, LANES), f32)
        stream[tiles + a, :, :width] = tail[:, a * LANES : a * LANES + width].astype(f32)
    local[4].wait()
    others = [lax.rem(me + step, count) for step in range(1, count)]
    for other in others:
        records_copy(other, other).wait_recv()

    inside = iota((FRAMES, LANES), 1) < LANES - HOP * (FRAMES - 1 - iota((FRAMES, LANES), 0))
    steps = [(g, c) for g in range(pieces) for c in range(tiles // chunk)]

    def arrive(g):
        span = slice(g * PIECE, (g + 1) * PIECE)
        columns = []
        for m in range(tiles):
            at = m * LANES % block_len
            columns.append(held[m * LANES // block_len, span, at : at + LANES])
            stream[m, span, :] = columns[m].astype(f32)
        for a in range(wide):
            columns.append(stream[tiles + a, span, :].astype(bf16))
        return columns

    def measure(index, columns):
        g, c = steps[index]
        at = index % 2 * PIECE * HOP
        scale, behind = scales(columns[c * chunk : (c + 1) * chunk + wide], window, order[...], band, level, at)
        for j, part in enumerate(end_taps(scale, behind, ends[g])):
            late[c, j + 1] += part

    def correlate(index):
        g, c = steps[index]
        sums = [None] * slots
        for b, s in enumerate(stations[g]):
            turned = [
                pltpu.roll(stream[c * chunk + m, pl.ds(s, FRAMES, stride=0), :], HOP, 1, stride=HOP, stride_axis=0)
                for m in range(chunk + wide)
            ]
            frames = [jnp.where(inside, turned[m], turned[m + 1]).astype(bf16) for m in range(chunk + wide - 1)]
            right = jnp.concatenate([jnp.concatenate(frames[a : a + chunk], axis=0) for a in range(wide)], axis=1)
            left = jnp.concatenate([shifts[s, a] for a in range(wide)], axis=1)
            corr = lax.dot_general(left, right, NT, preferred_element_type=f32)
            at = (index % 2 * PIECE + b) * HOP
            own_level = level[at : at + HOP, :]
            for k in range(slots):
                weight = own_level * coef[k, pl.ds(s, HOP, stride=0), :]
                term = corr[k * HOP : (k + 1) * HOP] * weight
                sums[k] = term if sums[k] is None else sums[k] + term
        for k in range(slots):
            acc[c, k * HOP : (k + 1) * HOP, :] += sums[k]

    columns = arrive(0)
    measure(0, columns)
    for index, (g, c) in enumerate(steps):
        if index + 1 < len(steps):
            if steps[index + 1][0] != g:
                columns = arrive(g + 1)
            measure(index + 1, columns)
        if c == 0 and g + early < pieces:
            build_shifts(temps, shifts, stations[g + early])
        correlate(index)

    per_half = slots // halves
    for c in range(tiles // chunk):
        for j in range(1, HOP):
            acc[c, pl.ds(j, slots, stride=HOP), :] += late[c, j]
        for h in range(halves):
            whole = [acc[c, k * HOP : (k + 1) * HOP, :] for k in range(h * per_half, (h + 1) * per_half)]
            for m, part in enumerate(swap_blocks(whole)):
                parts[c * chunk + m, h] = part

    everyone = [(other, core) for other in others]
    everyone += [
        (lax.rem(me + step, count), lax.rem(core + turn, halves)) for turn in range(1, halves) for step in range(count)
    ]
    sends = []
    per = tiles // count
    for step, (b, h) in enumerate(everyone):
        copy = pltpu.make_async_remote_copy(
            src_ref=parts.at[pl.ds(b * per, per), h],
            dst_ref=arrived.at[step],
            send_sem=out_send_sem.at[step],
            recv_sem=out_recv_sem.at[step],
            device_id={"tm": b, "sta": h},
            device_id_type=pl.DeviceIdType.MESH,
        )
        copy.start()
        sends.append(copy)
    total = parts[pl.ds(me * per, per), core]
    for step, copy in enumerate(sends):
        copy.wait_recv()
        total = total + arrived[step]
    mine = iota((HOP, LANES), 1) % HOP == iota((HOP, LANES), 0)
    for p in range(per):
        pieces = jnp.concatenate([piece.astype(f32) for piece in split(total[p], 3)], axis=0).astype(bf16)
        wider = jnp.dot(pieces, stretch[...], preferred_element_type=f32)
        wider = wider[:HOP] + wider[HOP : 2 * HOP] + wider[2 * HOP :]
        for k in range(per_half):
            line = jnp.where(mine, wider[:, k * LANES : (k + 1) * LANES], 0.0)
            out_ref[0, k : k + 1, p * LANES : (p + 1) * LANES] = jnp.sum(line, axis=0, keepdims=True)
    for copy in sends:
        copy.wait_send()
    for other in others:
        records_copy(other, me).wait_send()


def shards(count, halves, records, following, library, template_ids, channel_mask, station_group):
    block_len = records.shape[1]
    rows, window = library.shape[1:]
    batches, per_batch = template_ids.shape
    slots = template_ids.size
    wide = window // LANES
    tiles = count * block_len // LANES
    chunks = tiles * FRAMES // LANES
    peers = count * halves - 1
    pieces = rows // PIECE
    return pl.pallas_call(
        functools.partial(kernel, count, halves),
        in_specs=[pl.BlockSpec(memory_space=pl.ANY)] * 6,
        out_specs=pl.BlockSpec(memory_space=pltpu.VMEM),
        out_shape=jax.ShapeDtypeStruct((batches // halves, per_batch, block_len), f32),
        scratch_shapes=[
            pltpu.SMEM(template_ids.shape, template_ids.dtype),
            pltpu.VMEM(channel_mask.shape, channel_mask.dtype),
            pltpu.VMEM((1, station_group.shape[0]), station_group.dtype),
            pltpu.VMEM((count, rows, block_len), records.dtype),
            pltpu.VMEM((rows, following.shape[1]), following.dtype),
            pltpu.VMEM(library.shape, library.dtype),
            pltpu.VMEM((slots, wide, rows, LANES), f32),
            pltpu.VMEM((rows, wide, slots * HOP, LANES), bf16),
            pltpu.VMEM((tiles + wide, rows, LANES), f32),
            pltpu.VMEM((2 * PIECE * HOP, LANES), f32),
            pltpu.VMEM((slots, rows, LANES), f32),
            pltpu.VMEM((HOP * slots, LANES), f32),
            pltpu.VMEM((pieces, 2 * slots, HOP * PIECE), bf16),
            pltpu.VMEM((LANES, LANES), bf16),
            pltpu.VMEM((window + 2 * LANES, 2 * LANES), bf16),
            pltpu.VMEM((LANES, HOP * LANES), bf16),
            pltpu.VMEM((chunks, slots * HOP, LANES), f32),
            pltpu.VMEM((chunks, HOP, slots, LANES), f32),
            pltpu.VMEM((tiles, halves, HOP, LANES), f32),
            pltpu.VMEM((peers, tiles // count, HOP, LANES), f32),
            pltpu.SemaphoreType.DMA((6,)),
            pltpu.SemaphoreType.REGULAR((count // PAIR,)),
            pltpu.SemaphoreType.DMA((count,)),
            pltpu.SemaphoreType.DMA((count,)),
            pltpu.SemaphoreType.DMA((peers,)),
            pltpu.SemaphoreType.DMA((peers,)),
        ],
        compiler_params=pltpu.CompilerParams(collective_id=0, has_side_effects=True),
        name="matched_filter",
    )(template_ids, records, following, library, channel_mask, station_group.reshape(1, -1))


def solution(mesh):
    placed = (
        P("sta", ("days", "tm")),
        P("sta", "days"),
        P(None, ("sta", "tm"), None),
        P(),
        P(),
        P(),
    )
    return jax.shard_map(
        functools.partial(shards, mesh.shape["tm"], mesh.shape["sta"]),
        mesh=mesh,
        in_specs=placed,
        out_specs=P("sta", None, ("days", "tm")),
        check_vma=False,
    )
```

```python
import functools

import jax
import jax.numpy as jnp
from jax import lax
from jax.experimental import pallas as pl
from jax.experimental.pallas import tpu as pltpu
from jax.sharding import PartitionSpec as P

G = 128
LANES = 128
HOP = 8
FRAMES = LANES // HOP
PAIR = 2
PIECE = 64
EARLY = 1

epsilon = 1e-06

f32, bf16 = jnp.float32, jnp.bfloat16
NT = (((1,), (1,)), ((), ()))


def iota(shape, axis):
    return lax.broadcasted_iota(jnp.int32, shape, axis)


def as_bf16(mask):
    return mask.astype(f32).astype(bf16)


def split(x, count):
    pieces = []
    for _ in range(count):
        piece = x.astype(bf16)
        pieces.append(piece)
        x = x - piece.astype(f32)
    return pieces


def swap_blocks(tiles):
    block = iota(tiles[0].shape, 1) // FRAMES
    step = 1
    while step < len(tiles):
        odd = (block // step) % 2 == 1
        turned = list(tiles)
        for a in range(len(tiles)):
            if a & step == 0:
                low, high = tiles[a], tiles[a | step]
                turned[a] = jnp.where(odd, pltpu.roll(high, FRAMES * step, 1), low)
                turned[a | step] = jnp.where(odd, high, pltpu.roll(low, LANES - FRAMES * step, 1))
        tiles = turned
        step *= 2
    return tiles


def station_weights(ids, first, window, mask_ref, group_ref):
    stations = mask_ref.shape[1]
    turn = lax.rem(stations - first, stations)
    mask = jnp.concatenate([mask_ref[pl.ds(i, 1), :] for i in ids], axis=0).astype(f32)
    names = group_ref[...]
    onehot = iota((G, stations), 0) == jnp.broadcast_to(names, (G, stations))
    counts = lax.dot_general(mask.astype(bf16), as_bf16(onehot), NT, preferred_element_type=f32)
    mine = pltpu.roll(jnp.broadcast_to(names, (8, stations)), turn, 1)[:1, :LANES]
    chosen = as_bf16(iota((G, LANES), 0) == jnp.broadcast_to(mine, (G, LANES)))
    high = jnp.floor(counts / 128.0) * 128.0
    low = counts - high
    per_station = jnp.dot(high.astype(bf16), chosen, preferred_element_type=f32) + jnp.dot(
        low.astype(bf16), chosen, preferred_element_type=f32
    )
    my_mask = pltpu.roll(mask, turn, 1)[:, :LANES]
    return my_mask * lax.rsqrt(jnp.float32(window * G) * jnp.maximum(per_station, 1.0))


def pad_rows(x):
    if x.shape[0] == LANES:
        return x
    return jnp.concatenate([x, jnp.zeros((LANES - x.shape[0], x.shape[1]), x.dtype)], axis=0)


def spread_templates(ids, templates, temps, taps):
    slots, wide, rows, _ = temps.shape
    window = wide * LANES
    lane = iota((rows, LANES), 1)
    select = as_bf16(iota((16, LANES), 1) + iota((16, LANES), 0) == LANES)
    mean = jnp.zeros((rows, LANES), f32)
    for k in range(slots):
        template = templates[ids[k]]
        last = lax.dot_general(select, pad_rows(template[:, window - LANES :]), NT, preferred_element_type=f32)
        taps[pl.ds(k, HOP, stride=slots), :] = last[:HOP]
        template = template.astype(f32)
        for a in range(wide):
            temps[k, a] = template[:, a * LANES : (a + 1) * LANES]
        total = jnp.sum(template * template, axis=1, keepdims=True)
        mean = jnp.where(lane == k, total, mean)
    return mean


def weigh_templates(weights, mean, temps, coef, taps, ends):
    slots, wide, rows, _ = temps.shape
    window = wide * LANES
    mean = pad_rows(mean).T[:slots]
    own = weights * lax.rsqrt(mean / window + epsilon)
    pieces = jnp.concatenate(split(own, 3), axis=0)
    repeat = as_bf16(lax.rem(iota((3 * slots, slots * LANES), 0), slots) == iota((3 * slots, slots * LANES), 1) // LANES)
    spread = lax.dot_general(pieces, repeat, (((0,), (0,)), ((), ())), preferred_element_type=f32)
    for k in range(slots):
        coef[k] = spread[:rows, k * LANES : (k + 1) * LANES]
    piece = min(PIECE, rows)
    for g in range(rows // piece):
        tiles = [jnp.zeros((slots, LANES), f32)] * (HOP * piece // LANES)
        for d in range(1, HOP):
            place = (HOP - d) * piece
            part = taps[d * slots : (d + 1) * slots, :] * own
            part = pltpu.roll(part, (place - g * piece) % LANES, 1)
            at = place // LANES
            here = iota((slots, LANES), 1) // piece == (place % LANES) // piece
            tiles[at] = jnp.where(here, part, tiles[at])
        ends[g] = jnp.concatenate(split(jnp.concatenate(tiles, axis=1), 2), axis=0)


def build_shifts(temps, shifts, stations):
    slots, wide = temps.shape[:2]
    keep = iota((HOP, LANES), 1) >= iota((HOP, LANES), 0)
    for s in stations:
        columns = [[] for _ in range(wide)]
        for k in range(slots):
            before = jnp.zeros((HOP, LANES), f32)
            for a in range(wide):
                turned = pltpu.roll(temps[k, a, pl.ds(s, HOP, stride=0), :], 0, 1, stride=1, stride_axis=0)
                columns[a].append(jnp.where(keep, turned, before))
                before = turned
        for a in range(wide):
            shifts[s, a] = jnp.concatenate(columns[a], axis=0).astype(bf16)


def sample_at(lane):
    return HOP * (FRAMES - 1 - lane % FRAMES) + lane // FRAMES


def phase_order():
    return as_bf16(iota((LANES, LANES), 0) == sample_at(iota((LANES, LANES), 1)))


def band_matrix(window):
    shape = (window + 2 * LANES, 2 * LANES)
    column = iota(shape, 1)
    late = iota(shape, 0) - column // LANES * LANES - sample_at(column % LANES)
    return as_bf16(jnp.logical_and(late >= 0, late < window))


def stretch_matrix():
    row, lane = iota((LANES, HOP * LANES), 0), iota((LANES, HOP * LANES), 1)
    same = row // FRAMES == lane // LANES
    return as_bf16(jnp.logical_and(same, lane % LANES // HOP == FRAMES - 1 - row % FRAMES))


def scales(tiles, window, order, band, level, at):
    wide = window // LANES
    chunk = len(tiles) - wide
    stations = tiles[0].shape[0]
    mixed = jnp.dot(jnp.concatenate(tiles[wide:], axis=0), order, preferred_element_type=f32).astype(bf16)
    behind = swap_blocks([mixed[m * stations : (m + 1) * stations] for m in range(chunk)])
    squares = [tile.astype(f32) * tile.astype(f32) for tile in tiles]
    pieces = [split(square, 2) for square in squares]
    rows = [
        jnp.concatenate([pieces[m + a][half] for a in range(wide + 2)], axis=1)
        for half in range(2)
        for m in range(0, chunk, 2)
    ]
    sums = jnp.dot(jnp.concatenate(rows, axis=0), band[...], preferred_element_type=f32)
    count = chunk // 2 * stations
    scale = lax.rsqrt((sums[:count] + sums[count:]) / window + epsilon)
    scale = swap_blocks(
        [
            scale[m // 2 * stations : (m // 2 + 1) * stations, m % 2 * LANES : (m % 2 + 1) * LANES]
            for m in range(chunk)
        ]
    )
    for j in range(HOP):
        level[pl.ds(at + j, stations, stride=HOP), :] = scale[j]
    return scale, [part.astype(f32) for part in behind[: HOP - 1]]


def end_taps(scale, behind, ends):
    slots = ends.shape[0] // 2
    stations = scale[0].shape[0]
    zero = jnp.zeros((stations, LANES), f32)
    sums = []
    for j in range(1, HOP):
        blocks = HOP if j > HOP // 2 else HOP // 2
        parts = [scale[j] * behind[j - d] if d <= j else zero for d in range(blocks, 0, -1)]
        high, low = split(jnp.concatenate(parts, axis=0), 2)
        left = ends[:, (HOP - blocks) * stations :]
        some = jnp.dot(left, high, preferred_element_type=f32)
        more = jnp.dot(left[:slots], low, preferred_element_type=f32)
        sums.append(some[:slots] + some[slots:] + more)
    return sums


def kernel(
    count, halves,
    ids_ref, records_ref, following_ref, library_ref, mask_ref, group_ref,
    out_ref,
    ids_own, mask_own, group_own, held, tail, templates, temps, shifts, stream, level, coef, taps, ends,
    order, band, stretch, acc, late, parts, arrived,
    own_sem, meet_sem, send_sem, recv_sem, out_send_sem, out_recv_sem,
):
    me, core = lax.axis_index("tm"), lax.axis_index("sta")
    slots, wide, rows, _ = temps.shape
    window = wide * LANES
    block_len = held.shape[2]
    tiles = count * block_len // LANES
    chunk = LANES // FRAMES
    offset = pl.multiple_of(me * rows, rows)

    local = [
        pltpu.make_async_copy(ids_ref, ids_own, own_sem.at[0]),
        pltpu.make_async_copy(mask_ref, mask_own, own_sem.at[1]),
        pltpu.make_async_copy(group_ref, group_own, own_sem.at[2]),
        pltpu.make_async_copy(library_ref, templates, own_sem.at[3]),
        pltpu.make_async_copy(records_ref.at[pl.ds(offset, rows), :], held.at[me], own_sem.at[4]),
        pltpu.make_async_copy(following_ref.at[pl.ds(offset, rows), :], tail, own_sem.at[5]),
    ]
    for copy in local:
        copy.start()

    line = count // PAIR
    place, side = me // PAIR, lax.rem(me, PAIR)
    hops = [(None, me, lax.rem(core + turn, halves)) for turn in range(1, halves)]
    hops += [(None, place * PAIR + lax.rem(side + turn, PAIR), core) for turn in range(1, PAIR)]
    hops += [(place > 0, me - PAIR, core), (place < line - 1, me + PAIR, core)]
    degree = halves + PAIR - 2 + (place > 0).astype(jnp.int32) + (place < line - 1).astype(jnp.int32)

    def meeting(turn):
        return pltpu.get_barrier_semaphore() if turn == 0 else meet_sem.at[turn - 1]

    def greet(turn):
        for there, b, h in hops:
            def signal():
                pl.semaphore_signal(
                    meeting(turn), inc=1, device_id={"tm": b, "sta": h}, device_id_type=pl.DeviceIdType.MESH
                )
            if there is None:
                signal()
            else:
                pl.when(there)(signal)

    def meet(turn):
        pl.semaphore_wait(meeting(turn), degree)

    def records_copy(other, sender):
        return pltpu.make_async_remote_copy(
            src_ref=records_ref.at[pl.ds(pl.multiple_of(other * rows, rows), rows), :],
            dst_ref=held.at[sender],
            send_sem=send_sem.at[other],
            recv_sem=recv_sem.at[sender],
            device_id={"tm": other},
            device_id_type=pl.DeviceIdType.MESH,
        )

    def send(distance):
        for turn in range(PAIR):
            far = distance - (turn > 0)
            for step in sorted({far, -far}):
                if 0 <= far < line and (turn, step) != (0, 0):
                    other = (place + step) * PAIR + lax.rem(side + turn, PAIR)

                    def start(other=other):
                        records_copy(other, me).start()

                    if step == 0:
                        start()
                    else:
                        pl.when(jnp.logical_and(place + step >= 0, place + step < line))(start)

    greet(0)
    order[...] = phase_order()
    band[...] = band_matrix(window)
    stretch[...] = stretch_matrix()
    acc[...] = jnp.zeros(acc.shape, f32)
    late[...] = jnp.zeros(late.shape, f32)
    meet(0)
    greet(1)
    send(1)
    for copy in local[:3]:
        copy.wait()
    ids = [ids_own[j // ids_own.shape[1], j % ids_own.shape[1]] for j in range(slots)]
    first = core * (rows * count) + offset
    weights = station_weights(ids, first, window, mask_own, group_own)
    meet(1)
    greet(2)
    send(2)
    local[3].wait()
    mean = spread_templates(ids, templates, temps, taps)
    for turn in range(2, line + 1):
        meet(turn)
        if turn < line:
            greet(turn + 1)
            send(turn + 1)
        if turn == 2:
            weigh_templates(weights, mean, temps, coef, taps, ends)

    piece = min(PIECE, rows)
    pieces = rows // piece
    stations = [range(g * piece, (g + 1) * piece) for g in range(pieces)]
    early = min(EARLY, pieces)
    for g in range(early):
        build_shifts(temps, shifts, stations[g])
    local[5].wait()
    for a in range(wide):
        width = min(LANES, tail.shape[1] - a * LANES)
        stream[tiles + a] = jnp.zeros((rows, LANES), f32)
        stream[tiles + a, :, :width] = tail[:, a * LANES : a * LANES + width].astype(f32)
    local[4].wait()
    others = [lax.rem(me + step, count) for step in range(1, count)]
    for other in others:
        records_copy(other, other).wait_recv()

    inside = iota((FRAMES, LANES), 1) < LANES - HOP * (FRAMES - 1 - iota((FRAMES, LANES), 0))
    steps = [(g, c) for g in range(pieces) for c in range(tiles // chunk)]

    def arrive(g):
        span = slice(g * piece, (g + 1) * piece)
        columns = []
        for m in range(tiles):
            at = m * LANES % block_len
            columns.append(held[m * LANES // block_len, span, at : at + LANES])
            stream[m, span, :] = columns[m].astype(f32)
        for a in range(wide):
            columns.append(stream[tiles + a, span, :].astype(bf16))
        return columns

    def measure(index, columns):
        g, c = steps[index]
        at = index % 2 * piece * HOP
        scale, behind = scales(columns[c * chunk : (c + 1) * chunk + wide], window, order[...], band, level, at)
        for j, part in enumerate(end_taps(scale, behind, ends[g])):
            late[c, j + 1] += part

    def correlate(index):
        g, c = steps[index]
        sums = [None] * slots
        for b, s in enumerate(stations[g]):
            turned = [
                pltpu.roll(stream[c * chunk + m, pl.ds(s, FRAMES, stride=0), :], HOP, 1, stride=HOP, stride_axis=0)
                for m in range(chunk + wide)
            ]
            frames = [jnp.where(inside, turned[m], turned[m + 1]).astype(bf16) for m in range(chunk + wide - 1)]
            right = jnp.concatenate([jnp.concatenate(frames[a : a + chunk], axis=0) for a in range(wide)], axis=1)
            left = jnp.concatenate([shifts[s, a] for a in range(wide)], axis=1)
            corr = lax.dot_general(left, right, NT, preferred_element_type=f32)
            at = (index % 2 * piece + b) * HOP
            own_level = level[at : at + HOP, :]
            for k in range(slots):
                weight = own_level * coef[k, pl.ds(s, HOP, stride=0), :]
                term = corr[k * HOP : (k + 1) * HOP] * weight
                sums[k] = term if sums[k] is None else sums[k] + term
        for k in range(slots):
            acc[c, k * HOP : (k + 1) * HOP, :] += sums[k]

    columns = arrive(0)
    measure(0, columns)
    for index, (g, c) in enumerate(steps):
        if index + 1 < len(steps):
            if steps[index + 1][0] != g:
                columns = arrive(g + 1)
            measure(index + 1, columns)
        if c == 0 and g + early < pieces:
            build_shifts(temps, shifts, stations[g + early])
        correlate(index)

    per_half = slots // halves
    for c in range(tiles // chunk):
        for j in range(1, HOP):
            acc[c, pl.ds(j, slots, stride=HOP), :] += late[c, j]
        for h in range(halves):
            whole = [acc[c, k * HOP : (k + 1) * HOP, :] for k in range(h * per_half, (h + 1) * per_half)]
            for m, part in enumerate(swap_blocks(whole)):
                parts[c * chunk + m, h] = part

    everyone = [(other, core) for other in others]
    everyone += [
        (lax.rem(me + step, count), lax.rem(core + turn, halves)) for turn in range(1, halves) for step in range(count)
    ]
    sends = []
    per = tiles // count
    for step, (b, h) in enumerate(everyone):
        copy = pltpu.make_async_remote_copy(
            src_ref=parts.at[pl.ds(b * per, per), h],
            dst_ref=arrived.at[step],
            send_sem=out_send_sem.at[step],
            recv_sem=out_recv_sem.at[step],
            device_id={"tm": b, "sta": h},
            device_id_type=pl.DeviceIdType.MESH,
        )
        copy.start()
        sends.append(copy)
    total = parts[pl.ds(me * per, per), core]
    for step, copy in enumerate(sends):
        copy.wait_recv()
        total = total + arrived[step]
    mine = iota((HOP, LANES), 1) % HOP == iota((HOP, LANES), 0)
    for p in range(per):
        pieces = jnp.concatenate([piece.astype(f32) for piece in split(total[p], 3)], axis=0).astype(bf16)
        wider = jnp.dot(pieces, stretch[...], preferred_element_type=f32)
        wider = wider[:HOP] + wider[HOP : 2 * HOP] + wider[2 * HOP :]
        for k in range(per_half):
            line = jnp.where(mine, wider[:, k * LANES : (k + 1) * LANES], 0.0)
            out_ref[0, k : k + 1, p * LANES : (p + 1) * LANES] = jnp.sum(line, axis=0, keepdims=True)
    for copy in sends:
        copy.wait_send()
    for other in others:
        records_copy(other, me).wait_send()


def shards(count, halves, records, following, library, template_ids, channel_mask, station_group):
    block_len = records.shape[1]
    rows, window = library.shape[1:]
    batches, per_batch = template_ids.shape
    slots = template_ids.size
    wide = window // LANES
    tiles = count * block_len // LANES
    chunks = tiles * FRAMES // LANES
    peers = count * halves - 1
    piece = min(PIECE, rows)
    pieces = rows // piece
    return pl.pallas_call(
        functools.partial(kernel, count, halves),
        in_specs=[pl.BlockSpec(memory_space=pl.ANY)] * 6,
        out_specs=pl.BlockSpec(memory_space=pltpu.VMEM),
        out_shape=jax.ShapeDtypeStruct((batches // halves, per_batch, block_len), f32),
        scratch_shapes=[
            pltpu.SMEM(template_ids.shape, template_ids.dtype),
            pltpu.VMEM(channel_mask.shape, channel_mask.dtype),
            pltpu.VMEM((1, station_group.shape[0]), station_group.dtype),
            pltpu.VMEM((count, rows, block_len), records.dtype),
            pltpu.VMEM((rows, following.shape[1]), following.dtype),
            pltpu.VMEM(library.shape, library.dtype),
            pltpu.VMEM((slots, wide, rows, LANES), f32),
            pltpu.VMEM((rows, wide, slots * HOP, LANES), bf16),
            pltpu.VMEM((tiles + wide, rows, LANES), f32),
            pltpu.VMEM((2 * piece * HOP, LANES), f32),
            pltpu.VMEM((slots, rows, LANES), f32),
            pltpu.VMEM((HOP * slots, LANES), f32),
            pltpu.VMEM((pieces, 2 * slots, HOP * piece), bf16),
            pltpu.VMEM((LANES, LANES), bf16),
            pltpu.VMEM((window + 2 * LANES, 2 * LANES), bf16),
            pltpu.VMEM((LANES, HOP * LANES), bf16),
            pltpu.VMEM((chunks, slots * HOP, LANES), f32),
            pltpu.VMEM((chunks, HOP, slots, LANES), f32),
            pltpu.VMEM((tiles, halves, HOP, LANES), f32),
            pltpu.VMEM((peers, tiles // count, HOP, LANES), f32),
            pltpu.SemaphoreType.DMA((6,)),
            pltpu.SemaphoreType.REGULAR((count // PAIR,)),
            pltpu.SemaphoreType.DMA((count,)),
            pltpu.SemaphoreType.DMA((count,)),
            pltpu.SemaphoreType.DMA((peers,)),
            pltpu.SemaphoreType.DMA((peers,)),
        ],
        compiler_params=pltpu.CompilerParams(collective_id=0, has_side_effects=True),
        name="matched_filter",
    )(template_ids, records, following, library, channel_mask, station_group.reshape(1, -1))


def solution(mesh):
    placed = (
        P("sta", ("days", "tm")),
        P("sta", "days"),
        P(None, ("sta", "tm"), None),
        P(),
        P(),
        P(),
    )
    return jax.shard_map(
        functools.partial(shards, mesh.shape["tm"], mesh.shape["sta"]),
        mesh=mesh,
        in_specs=placed,
        out_specs=P("sta", None, ("days", "tm")),
        check_vma=False,
    )
```

```python
import functools

import jax
import jax.numpy as jnp
from jax import lax
from jax.experimental import pallas as pl
from jax.experimental.pallas import tpu as pltpu
from jax.sharding import PartitionSpec as P

G = 128
LANES = 128
HOP = 8
FRAMES = LANES // HOP
PAIR = 2
PIECE = 128
EARLY = 1

epsilon = 1e-06

f32, bf16 = jnp.float32, jnp.bfloat16
NT = (((1,), (1,)), ((), ()))


def iota(shape, axis):
    return lax.broadcasted_iota(jnp.int32, shape, axis)


def as_bf16(mask):
    return mask.astype(f32).astype(bf16)


def split(x, count):
    pieces = []
    for _ in range(count):
        piece = x.astype(bf16)
        pieces.append(piece)
        x = x - piece.astype(f32)
    return pieces


def swap_blocks(tiles):
    block = iota(tiles[0].shape, 1) // FRAMES
    step = 1
    while step < len(tiles):
        odd = (block // step) % 2 == 1
        turned = list(tiles)
        for a in range(len(tiles)):
            if a & step == 0:
                low, high = tiles[a], tiles[a | step]
                turned[a] = jnp.where(odd, pltpu.roll(high, FRAMES * step, 1), low)
                turned[a | step] = jnp.where(odd, high, pltpu.roll(low, LANES - FRAMES * step, 1))
        tiles = turned
        step *= 2
    return tiles


def station_weights(ids, first, window, mask_ref, group_ref):
    stations = mask_ref.shape[1]
    turn = lax.rem(stations - first, stations)
    mask = jnp.concatenate([mask_ref[pl.ds(i, 1), :] for i in ids], axis=0).astype(f32)
    names = group_ref[...]
    onehot = iota((G, stations), 0) == jnp.broadcast_to(names, (G, stations))
    counts = lax.dot_general(mask.astype(bf16), as_bf16(onehot), NT, preferred_element_type=f32)
    mine = pltpu.roll(jnp.broadcast_to(names, (8, stations)), turn, 1)[:1, :LANES]
    chosen = as_bf16(iota((G, LANES), 0) == jnp.broadcast_to(mine, (G, LANES)))
    high = jnp.floor(counts / 128.0) * 128.0
    low = counts - high
    per_station = jnp.dot(high.astype(bf16), chosen, preferred_element_type=f32) + jnp.dot(
        low.astype(bf16), chosen, preferred_element_type=f32
    )
    my_mask = pltpu.roll(mask, turn, 1)[:, :LANES]
    return my_mask * lax.rsqrt(jnp.float32(window * G) * jnp.maximum(per_station, 1.0))


def pad_rows(x):
    if x.shape[0] == LANES:
        return x
    return jnp.concatenate([x, jnp.zeros((LANES - x.shape[0], x.shape[1]), x.dtype)], axis=0)


def spread_templates(ids, templates, temps, taps):
    slots, wide, rows, _ = temps.shape
    window = wide * LANES
    lane = iota((rows, LANES), 1)
    select = as_bf16(iota((16, LANES), 1) + iota((16, LANES), 0) == LANES)
    mean = jnp.zeros((rows, LANES), f32)
    for k in range(slots):
        template = templates[ids[k]]
        last = lax.dot_general(select, pad_rows(template[:, window - LANES :]), NT, preferred_element_type=f32)
        taps[pl.ds(k, HOP, stride=slots), :] = last[:HOP]
        template = template.astype(f32)
        for a in range(wide):
            temps[k, a] = template[:, a * LANES : (a + 1) * LANES]
        total = jnp.sum(template * template, axis=1, keepdims=True)
        mean = jnp.where(lane == k, total, mean)
    return mean


def weigh_templates(weights, mean, temps, coef, taps, ends):
    slots, wide, rows, _ = temps.shape
    window = wide * LANES
    mean = pad_rows(mean).T[:slots]
    own = weights * lax.rsqrt(mean / window + epsilon)
    pieces = jnp.concatenate(split(own, 3), axis=0)
    repeat = as_bf16(lax.rem(iota((3 * slots, slots * LANES), 0), slots) == iota((3 * slots, slots * LANES), 1) // LANES)
    spread = lax.dot_general(pieces, repeat, (((0,), (0,)), ((), ())), preferred_element_type=f32)
    for k in range(slots):
        coef[k] = spread[:rows, k * LANES : (k + 1) * LANES]
    piece = min(PIECE, rows)
    for g in range(rows // piece):
        tiles = [jnp.zeros((slots, LANES), f32)] * (HOP * piece // LANES)
        for d in range(1, HOP):
            place = (HOP - d) * piece
            part = taps[d * slots : (d + 1) * slots, :] * own
            part = pltpu.roll(part, (place - g * piece) % LANES, 1)
            at = place // LANES
            here = iota((slots, LANES), 1) // piece == (place % LANES) // piece
            tiles[at] = jnp.where(here, part, tiles[at])
        ends[g] = jnp.concatenate(split(jnp.concatenate(tiles, axis=1), 2), axis=0)


def build_shifts(temps, shifts, stations):
    slots, wide = temps.shape[:2]
    keep = iota((HOP, LANES), 1) >= iota((HOP, LANES), 0)
    for s in stations:
        columns = [[] for _ in range(wide)]
        for k in range(slots):
            before = jnp.zeros((HOP, LANES), f32)
            for a in range(wide):
                turned = pltpu.roll(temps[k, a, pl.ds(s, HOP, stride=0), :], 0, 1, stride=1, stride_axis=0)
                columns[a].append(jnp.where(keep, turned, before))
                before = turned
        for a in range(wide):
            shifts[s, a] = jnp.concatenate(columns[a], axis=0).astype(bf16)


def sample_at(lane):
    return HOP * (FRAMES - 1 - lane % FRAMES) + lane // FRAMES


def phase_order():
    return as_bf16(iota((LANES, LANES), 0) == sample_at(iota((LANES, LANES), 1)))


def band_matrix(window):
    shape = (window + 2 * LANES, 2 * LANES)
    column = iota(shape, 1)
    late = iota(shape, 0) - column // LANES * LANES - sample_at(column % LANES)
    return as_bf16(jnp.logical_and(late >= 0, late < window))


def stretch_matrix():
    row, lane = iota((LANES, HOP * LANES), 0), iota((LANES, HOP * LANES), 1)
    same = row // FRAMES == lane // LANES
    return as_bf16(jnp.logical_and(same, lane % LANES // HOP == FRAMES - 1 - row % FRAMES))


def scales(tiles, window, order, band, level, at):
    wide = window // LANES
    chunk = len(tiles) - wide
    stations = tiles[0].shape[0]
    mixed = jnp.dot(jnp.concatenate(tiles[wide:], axis=0), order, preferred_element_type=f32).astype(bf16)
    behind = swap_blocks([mixed[m * stations : (m + 1) * stations] for m in range(chunk)])
    squares = [tile.astype(f32) * tile.astype(f32) for tile in tiles]
    pieces = [split(square, 2) for square in squares]
    rows = [
        jnp.concatenate([pieces[m + a][half] for a in range(wide + 2)], axis=1)
        for half in range(2)
        for m in range(0, chunk, 2)
    ]
    sums = jnp.dot(jnp.concatenate(rows, axis=0), band[...], preferred_element_type=f32)
    count = chunk // 2 * stations
    scale = lax.rsqrt((sums[:count] + sums[count:]) / window + epsilon)
    scale = swap_blocks(
        [
            scale[m // 2 * stations : (m // 2 + 1) * stations, m % 2 * LANES : (m % 2 + 1) * LANES]
            for m in range(chunk)
        ]
    )
    for j in range(HOP):
        level[pl.ds(at + j, stations, stride=HOP), :] = scale[j]
    return scale, [part.astype(f32) for part in behind[: HOP - 1]]


def end_taps(scale, behind, ends):
    slots = ends.shape[0] // 2
    stations = scale[0].shape[0]
    zero = jnp.zeros((stations, LANES), f32)
    sums = []
    for j in range(1, HOP):
        blocks = HOP if j > HOP // 2 else HOP // 2
        parts = [scale[j] * behind[j - d] if d <= j else zero for d in range(blocks, 0, -1)]
        high, low = split(jnp.concatenate(parts, axis=0), 2)
        left = ends[:, (HOP - blocks) * stations :]
        some = jnp.dot(left, high, preferred_element_type=f32)
        more = jnp.dot(left[:slots], low, preferred_element_type=f32)
        sums.append(some[:slots] + some[slots:] + more)
    return sums


def kernel(
    count, halves,
    ids_ref, records_ref, following_ref, library_ref, mask_ref, group_ref,
    out_ref,
    ids_own, mask_own, group_own, held, tail, templates, temps, shifts, stream, level, coef, taps, ends,
    order, band, stretch, acc, late, parts, arrived,
    own_sem, meet_sem, send_sem, recv_sem, out_send_sem, out_recv_sem,
):
    me, core = lax.axis_index("tm"), lax.axis_index("sta")
    slots, wide, rows, _ = temps.shape
    window = wide * LANES
    block_len = held.shape[2]
    tiles = count * block_len // LANES
    chunk = LANES // FRAMES
    offset = pl.multiple_of(me * rows, rows)

    local = [
        pltpu.make_async_copy(ids_ref, ids_own, own_sem.at[0]),
        pltpu.make_async_copy(mask_ref, mask_own, own_sem.at[1]),
        pltpu.make_async_copy(group_ref, group_own, own_sem.at[2]),
        pltpu.make_async_copy(library_ref, templates, own_sem.at[3]),
        pltpu.make_async_copy(records_ref.at[pl.ds(offset, rows), :], held.at[me], own_sem.at[4]),
        pltpu.make_async_copy(following_ref.at[pl.ds(offset, rows), :], tail, own_sem.at[5]),
    ]
    for copy in local:
        copy.start()

    line = count // PAIR
    place, side = me // PAIR, lax.rem(me, PAIR)
    hops = [(None, me, lax.rem(core + turn, halves)) for turn in range(1, halves)]
    hops += [(None, place * PAIR + lax.rem(side + turn, PAIR), core) for turn in range(1, PAIR)]
    hops += [(place > 0, me - PAIR, core), (place < line - 1, me + PAIR, core)]
    degree = halves + PAIR - 2 + (place > 0).astype(jnp.int32) + (place < line - 1).astype(jnp.int32)

    def meeting(turn):
        return pltpu.get_barrier_semaphore() if turn == 0 else meet_sem.at[turn - 1]

    def greet(turn):
        for there, b, h in hops:
            def signal():
                pl.semaphore_signal(
                    meeting(turn), inc=1, device_id={"tm": b, "sta": h}, device_id_type=pl.DeviceIdType.MESH
                )
            if there is None:
                signal()
            else:
                pl.when(there)(signal)

    def meet(turn):
        pl.semaphore_wait(meeting(turn), degree)

    def records_copy(other, sender):
        return pltpu.make_async_remote_copy(
            src_ref=records_ref.at[pl.ds(pl.multiple_of(other * rows, rows), rows), :],
            dst_ref=held.at[sender],
            send_sem=send_sem.at[other],
            recv_sem=recv_sem.at[sender],
            device_id={"tm": other},
            device_id_type=pl.DeviceIdType.MESH,
        )

    def send(distance):
        for turn in range(PAIR):
            far = distance - (turn > 0)
            for step in sorted({far, -far}):
                if 0 <= far < line and (turn, step) != (0, 0):
                    other = (place + step) * PAIR + lax.rem(side + turn, PAIR)

                    def start(other=other):
                        records_copy(other, me).start()

                    if step == 0:
                        start()
                    else:
                        pl.when(jnp.logical_and(place + step >= 0, place + step < line))(start)

    greet(0)
    order[...] = phase_order()
    band[...] = band_matrix(window)
    stretch[...] = stretch_matrix()
    acc[...] = jnp.zeros(acc.shape, f32)
    late[...] = jnp.zeros(late.shape, f32)
    meet(0)
    greet(1)
    send(1)
    for copy in local[:3]:
        copy.wait()
    ids = [ids_own[j // ids_own.shape[1], j % ids_own.shape[1]] for j in range(slots)]
    first = core * (rows * count) + offset
    weights = station_weights(ids, first, window, mask_own, group_own)
    meet(1)
    greet(2)
    send(2)
    local[3].wait()
    mean = spread_templates(ids, templates, temps, taps)
    for turn in range(2, line + 1):
        meet(turn)
        if turn < line:
            greet(turn + 1)
            send(turn + 1)
        if turn == 2:
            weigh_templates(weights, mean, temps, coef, taps, ends)

    piece = min(PIECE, rows)
    pieces = rows // piece
    stations = [range(g * piece, (g + 1) * piece) for g in range(pieces)]
    early = min(EARLY, pieces)
    for g in range(early):
        build_shifts(temps, shifts, stations[g])
    local[5].wait()
    for a in range(wide):
        width = min(LANES, tail.shape[1] - a * LANES)
        stream[tiles + a] = jnp.zeros((rows, LANES), f32)
        stream[tiles + a, :, :width] = tail[:, a * LANES : a * LANES + width].astype(f32)
    local[4].wait()
    others = [lax.rem(me + step, count) for step in range(1, count)]
    for other in others:
        records_copy(other, other).wait_recv()

    inside = iota((FRAMES, LANES), 1) < LANES - HOP * (FRAMES - 1 - iota((FRAMES, LANES), 0))
    steps = [(g, c) for g in range(pieces) for c in range(tiles // chunk)]

    def arrive(g):
        span = slice(g * piece, (g + 1) * piece)
        columns = []
        for m in range(tiles):
            at = m * LANES % block_len
            columns.append(held[m * LANES // block_len, span, at : at + LANES])
            stream[m, span, :] = columns[m].astype(f32)
        for a in range(wide):
            columns.append(stream[tiles + a, span, :].astype(bf16))
        return columns

    def measure(index, columns):
        g, c = steps[index]
        at = index % 2 * piece * HOP
        scale, behind = scales(columns[c * chunk : (c + 1) * chunk + wide], window, order[...], band, level, at)
        for j, part in enumerate(end_taps(scale, behind, ends[g])):
            late[c, j + 1] += part

    def correlate(index):
        g, c = steps[index]
        sums = [None] * slots
        for b, s in enumerate(stations[g]):
            turned = [
                pltpu.roll(stream[c * chunk + m, pl.ds(s, FRAMES, stride=0), :], HOP, 1, stride=HOP, stride_axis=0)
                for m in range(chunk + wide)
            ]
            frames = [jnp.where(inside, turned[m], turned[m + 1]).astype(bf16) for m in range(chunk + wide - 1)]
            right = jnp.concatenate([jnp.concatenate(frames[a : a + chunk], axis=0) for a in range(wide)], axis=1)
            left = jnp.concatenate([shifts[s, a] for a in range(wide)], axis=1)
            corr = lax.dot_general(left, right, NT, preferred_element_type=f32)
            at = (index % 2 * piece + b) * HOP
            own_level = level[at : at + HOP, :]
            for k in range(slots):
                weight = own_level * coef[k, pl.ds(s, HOP, stride=0), :]
                term = corr[k * HOP : (k + 1) * HOP] * weight
                sums[k] = term if sums[k] is None else sums[k] + term
        for k in range(slots):
            acc[c, k * HOP : (k + 1) * HOP, :] += sums[k]

    columns = arrive(0)
    measure(0, columns)
    for index, (g, c) in enumerate(steps):
        if index + 1 < len(steps):
            if steps[index + 1][0] != g:
                columns = arrive(g + 1)
            measure(index + 1, columns)
        if c == 0 and g + early < pieces:
            build_shifts(temps, shifts, stations[g + early])
        correlate(index)

    per_half = slots // halves
    for c in range(tiles // chunk):
        for j in range(1, HOP):
            acc[c, pl.ds(j, slots, stride=HOP), :] += late[c, j]
        for h in range(halves):
            whole = [acc[c, k * HOP : (k + 1) * HOP, :] for k in range(h * per_half, (h + 1) * per_half)]
            for m, part in enumerate(swap_blocks(whole)):
                parts[c * chunk + m, h] = part

    everyone = [(other, core) for other in others]
    everyone += [
        (lax.rem(me + step, count), lax.rem(core + turn, halves)) for turn in range(1, halves) for step in range(count)
    ]
    sends = []
    per = tiles // count
    for step, (b, h) in enumerate(everyone):
        copy = pltpu.make_async_remote_copy(
            src_ref=parts.at[pl.ds(b * per, per), h],
            dst_ref=arrived.at[step],
            send_sem=out_send_sem.at[step],
            recv_sem=out_recv_sem.at[step],
            device_id={"tm": b, "sta": h},
            device_id_type=pl.DeviceIdType.MESH,
        )
        copy.start()
        sends.append(copy)
    total = parts[pl.ds(me * per, per), core]
    for step, copy in enumerate(sends):
        copy.wait_recv()
        total = total + arrived[step]
    mine = iota((HOP, LANES), 1) % HOP == iota((HOP, LANES), 0)
    for p in range(per):
        pieces = jnp.concatenate([piece.astype(f32) for piece in split(total[p], 3)], axis=0).astype(bf16)
        wider = jnp.dot(pieces, stretch[...], preferred_element_type=f32)
        wider = wider[:HOP] + wider[HOP : 2 * HOP] + wider[2 * HOP :]
        for k in range(per_half):
            line = jnp.where(mine, wider[:, k * LANES : (k + 1) * LANES], 0.0)
            out_ref[0, k : k + 1, p * LANES : (p + 1) * LANES] = jnp.sum(line, axis=0, keepdims=True)
    for copy in sends:
        copy.wait_send()
    for other in others:
        records_copy(other, me).wait_send()


def shards(count, halves, records, following, library, template_ids, channel_mask, station_group):
    block_len = records.shape[1]
    rows, window = library.shape[1:]
    batches, per_batch = template_ids.shape
    slots = template_ids.size
    wide = window // LANES
    tiles = count * block_len // LANES
    chunks = tiles * FRAMES // LANES
    peers = count * halves - 1
    piece = min(PIECE, rows)
    pieces = rows // piece
    return pl.pallas_call(
        functools.partial(kernel, count, halves),
        in_specs=[pl.BlockSpec(memory_space=pl.ANY)] * 6,
        out_specs=pl.BlockSpec(memory_space=pltpu.VMEM),
        out_shape=jax.ShapeDtypeStruct((batches // halves, per_batch, block_len), f32),
        scratch_shapes=[
            pltpu.SMEM(template_ids.shape, template_ids.dtype),
            pltpu.VMEM(channel_mask.shape, channel_mask.dtype),
            pltpu.VMEM((1, station_group.shape[0]), station_group.dtype),
            pltpu.VMEM((count, rows, block_len), records.dtype),
            pltpu.VMEM((rows, following.shape[1]), following.dtype),
            pltpu.VMEM(library.shape, library.dtype),
            pltpu.VMEM((slots, wide, rows, LANES), f32),
            pltpu.VMEM((rows, wide, slots * HOP, LANES), bf16),
            pltpu.VMEM((tiles + wide, rows, LANES), f32),
            pltpu.VMEM((2 * piece * HOP, LANES), f32),
            pltpu.VMEM((slots, rows, LANES), f32),
            pltpu.VMEM((HOP * slots, LANES), f32),
            pltpu.VMEM((pieces, 2 * slots, HOP * piece), bf16),
            pltpu.VMEM((LANES, LANES), bf16),
            pltpu.VMEM((window + 2 * LANES, 2 * LANES), bf16),
            pltpu.VMEM((LANES, HOP * LANES), bf16),
            pltpu.VMEM((chunks, slots * HOP, LANES), f32),
            pltpu.VMEM((chunks, HOP, slots, LANES), f32),
            pltpu.VMEM((tiles, halves, HOP, LANES), f32),
            pltpu.VMEM((peers, tiles // count, HOP, LANES), f32),
            pltpu.SemaphoreType.DMA((6,)),
            pltpu.SemaphoreType.REGULAR((count // PAIR,)),
            pltpu.SemaphoreType.DMA((count,)),
            pltpu.SemaphoreType.DMA((count,)),
            pltpu.SemaphoreType.DMA((peers,)),
            pltpu.SemaphoreType.DMA((peers,)),
        ],
        compiler_params=pltpu.CompilerParams(collective_id=0, has_side_effects=True),
        name="matched_filter",
    )(template_ids, records, following, library, channel_mask, station_group.reshape(1, -1))


def solution(mesh):
    placed = (
        P("sta", ("days", "tm")),
        P("sta", "days"),
        P(None, ("sta", "tm"), None),
        P(),
        P(),
        P(),
    )
    return jax.shard_map(
        functools.partial(shards, mesh.shape["tm"], mesh.shape["sta"]),
        mesh=mesh,
        in_specs=placed,
        out_specs=P("sta", None, ("days", "tm")),
        check_vma=False,
    )
```
